32 devices in a mesh: row: 4 (over z), col: 8 (over y, x, core).
Axes of the slice: x: 2, y: 2, z: 4, core: 2. Of those that a mesh axis runs over, the one named last changes fastest.
Arguments:
- symmetric: float32 [16384, 16384], P('row', 'col'), may hold values from -8 to 8, as said below
- reflectors: float32 [4, 64, 16384], P(None, None, ('row', 'col')), may hold values from -0.125 to 0.125
- tri_factor: float32 [4, 64, 64], replicated, may hold values from -0.4 to 1.5, as said below
Outputs:
- updated: float32 [16384, 16384], P('row', 'col')
The draws below stay inside these ranges and needn't reach their ends.
Inputs may be any that keep to these rules, and one draw needn't show every extreme that they name: symmetric is a symmetric matrix. Each tri_factor[p] is upper triangular.
All inputs are finite; a program needn't handle non-finite values.
Results may differ from the reference program's by a relative error of at most 0.00029.
Values sent between devices are 32-bit elements; how exact they have to be, the bound alone decides.
No kernel may reach another device: no remote copies, remote signals or barrier semaphores. Data moves between devices by JAX's collectives and lax.ppermute only.
A program may use at most 128 MiB of HBM per device.

```python
import jax
import jax.numpy as jnp
from jax import lax

N = 16384
NB = 64
PANELS = 4


def draw_symmetric(key, part):
    base = jax.random.normal(key, (N, N), jnp.float32)
    paired = (base + base.T) * 0.70710678
    return jnp.clip(paired, -8.0, 8.0)


def draw_tri_factor(key, part):
    first = jax.random.fold_in(key, 11)
    second = jax.random.fold_in(key, 13)
    diagonal = jax.random.uniform(first, (PANELS, NB), jnp.float32, 0.6, 1.4)
    spread = jnp.clip(0.1 * jax.random.normal(second, (PANELS, NB, NB), jnp.float32), -0.4, 0.4)
    return jnp.triu(spread, 1) + diagonal[:, :, None] * jnp.eye(NB, dtype=jnp.float32)[None, :, :]


def block_levels(stream_key, dims, pieces, low, largest):
    def one(position, blocks):
        heights = jax.random.uniform(jax.random.fold_in(jax.random.fold_in(stream_key, 6), position), (blocks,), jnp.float32, low / len(pieces), largest / len(pieces))
        return jnp.repeat(jnp.exp(heights), dims[position] // blocks).reshape((-1,) + (1,) * (len(dims) - position - 1))

    gain = one(*pieces[0])
    for cut in pieces[1:]:
        gain = gain * one(*cut)
    return gain


def noise(rng, extent, scale, most, split=(), held_as=jnp.bfloat16):
    factor_of = block_levels(rng, extent, split, -0.22, 0.18) if split else 1.0
    drawn = jax.random.normal(rng, extent, jnp.float32) * scale * factor_of
    return jnp.minimum(jnp.maximum(drawn, -most), most).astype(held_as)


def setup_inputs(seed: int = 0) -> dict:
    key_of = jax.random.split(jax.random.key(seed), 4)
    symmetric = draw_symmetric(jax.random.fold_in(key_of[3], 71), 0)
    reflectors = noise(key_of[1], (PANELS, NB, N), (N // 8) ** -0.5, 0.125, ((2, 32),), jnp.float32)
    tri_factor = draw_tri_factor(jax.random.fold_in(key_of[3], 71), 0)
    return {"symmetric": symmetric, "reflectors": reflectors, "tri_factor": tri_factor}


def reference(symmetric, reflectors, tri_factor):
    highest = lax.Precision.HIGHEST
    matrix = symmetric
    for panel in range(PANELS):
        reflect = reflectors[panel]
        factor = tri_factor[panel]
        product = lax.dot_general(reflect, matrix, (((1,), (1,)), ((), ())), precision=highest, preferred_element_type=jnp.float32)
        image = jnp.dot(factor.T, product, precision=highest, preferred_element_type=jnp.float32)
        inner = lax.dot_general(reflect, image, (((1,), (1,)), ((), ())), precision=highest, preferred_element_type=jnp.float32)
        coupling = jnp.dot(factor.T, inner, precision=highest, preferred_element_type=jnp.float32)
        update = image - 0.5 * jnp.dot(coupling.T, reflect, precision=highest, preferred_element_type=jnp.float32)
        left_block = jnp.concatenate([reflect, update], axis=0)
        right_block = jnp.concatenate([update, reflect], axis=0)
        matrix = matrix - lax.dot_general(left_block, right_block, (((0,), (0,)), ((), ())), precision=highest, preferred_element_type=jnp.float32)
    return matrix
```

```python
import functools

import jax
import jax.numpy as jnp
from jax import lax
from jax.experimental import pallas as pl
from jax.experimental.pallas import tpu as pltpu
from jax.sharding import PartitionSpec as P


F32 = jnp.float32
BF16 = jnp.bfloat16
LANES = 128
VMEM_LIMIT = 60 * 1024 * 1024
NN = ((1,), (0,))
NT = ((1,), (1,))
TN = ((0,), (0,))


def split(value):
    high = value.astype(BF16)
    return high, (value - high.astype(F32)).astype(BF16)


def dot_split(left, right, dims):
    def part(a, b):
        return lax.dot_general(a, b, (dims, ((), ())), preferred_element_type=F32)

    return part(left[0], right[0]) + (part(left[0], right[1]) + part(left[1], right[0]))


def dot_full(a, b, dims=NN):
    return lax.dot_general(
        a, b, (dims, ((), ())), precision=lax.Precision.HIGHEST, preferred_element_type=F32
    )


def params():
    return pltpu.CompilerParams(vmem_limit_bytes=VMEM_LIMIT)


def cost(flops, bytes_accessed):
    return pl.CostEstimate(flops=flops, bytes_accessed=bytes_accessed, transcendentals=0)


def anywhere(count):
    return [pl.BlockSpec(memory_space=pl.ANY)] * count


def exchange(value, offset, count):
    return lax.ppermute(value, "col", [(i, i ^ offset) for i in range(count)])


def ring_shift(value, ring):
    size = len(ring)
    return lax.ppermute(value, "row", [(ring[i], ring[(i + 1) % size]) for i in range(size)])


def fetch(refs, buffer, sems):
    for i, ref in enumerate(refs):
        pltpu.make_async_copy(ref, buffer.at[i], sems.at[i]).start()


def await_fetch(ref, buffer, sems, i):
    pltpu.make_async_copy(ref, buffer.at[i], sems.at[i]).wait()


def columns_kernel(count, pieces, width, table, *refs):
    vs, m_ref, outs, (buffer, sems) = refs[:count], refs[count], refs[count + 1 : -2], refs[-2:]
    step = pl.program_id(0)

    @pl.when(step == 0)
    def _():
        fetch(vs, buffer, sems)

    await_fetch(vs[0], buffer, sems, step)
    left = split(buffer[step])
    for i in range(pieces):
        at = pl.multiple_of(table[1, i] * width, width)
        total = dot_split(left, split(m_ref[:, pl.ds(at, width)]), NN)

        @pl.when(step == 0)
        def _():
            outs[i][...] = total

        @pl.when(step > 0)
        def _():
            outs[i][...] += total


def product_columns(table, vs, matrix, pieces):
    count = len(vs)
    vectors, tile = vs[0].shape
    cols = matrix.shape[1]
    width = cols // pieces
    piece = pl.BlockSpec((vectors, width), lambda s, t: (0, 0))
    return pl.pallas_call(
        functools.partial(columns_kernel, count, pieces, width),
        out_shape=[jax.ShapeDtypeStruct((vectors, width), F32)] * pieces,
        grid_spec=pltpu.PrefetchScalarGridSpec(
            num_scalar_prefetch=1,
            grid=(count,),
            in_specs=anywhere(count) + [pl.BlockSpec((tile, cols), lambda s, t: (t[0, s], 0))],
            out_specs=[piece] * pieces,
            scratch_shapes=[pltpu.VMEM((count, vectors, tile), F32), pltpu.SemaphoreType.DMA((count,))],
        ),
        compiler_params=params(),
        cost_estimate=cost(6 * count * tile * cols * vectors, 4 * count * tile * cols),
        name="product_columns",
    )(table, *vs, matrix)


def rows_kernel(pieces, width, more, table, *refs):
    vcs, refs = refs[:pieces], refs[pieces:]
    m_ref, refs = refs[0], refs[1:]
    before, (out_ref, buffer, high_ref, low_ref, sems) = refs[:more], refs[more:]

    @pl.when(pl.program_id(0) == 0)
    def _():
        fetch(vcs, buffer, sems)
        for k in range(pieces):
            await_fetch(vcs[k], buffer, sems, k)
            high_ref[k], low_ref[k] = split(buffer[k])

    total = before[0][0] if more else None
    for k in range(pieces):
        at = pl.multiple_of(table[2, k] * width, width)
        left = split(m_ref[:, pl.ds(at, width)])
        term = dot_split(left, (high_ref[k], low_ref[k]), NT)
        total = term if total is None else total + term
    out_ref[0] = total


def product_rows(table, first, count, vcs, matrix, before=()):
    pieces = len(vcs)
    vectors, width = vcs[0].shape
    rows, cols = matrix.shape
    tile = rows // (2 * count)
    entry = pl.BlockSpec((1, tile, vectors), lambda s, t: (s, 0, 0))
    return pl.pallas_call(
        functools.partial(rows_kernel, pieces, width, len(before)),
        out_shape=jax.ShapeDtypeStruct((count, tile, vectors), F32),
        grid_spec=pltpu.PrefetchScalarGridSpec(
            num_scalar_prefetch=1,
            grid=(count,),
            in_specs=anywhere(pieces)
            + [pl.BlockSpec((tile, cols), lambda s, t: (t[0, first + s], 0))]
            + [entry] * len(before),
            out_specs=entry,
            scratch_shapes=[pltpu.VMEM((pieces, vectors, width), F32)]
            + [pltpu.VMEM((pieces, vectors, width), BF16)] * 2
            + [pltpu.SemaphoreType.DMA((pieces,))],
        ),
        compiler_params=params(),
        cost_estimate=cost(6 * count * tile * cols * vectors, 4 * count * tile * cols),
        name="product_rows",
    )(table, *vcs, matrix, *before)


def inner_kernel(pieces, nb, table, own_ref, *refs):
    vcs, pcs, out_ref = refs[:pieces], refs[pieces : 2 * pieces], refs[2 * pieces]
    buffer, sems = refs[2 * pieces + 1 :]
    fetch(vcs, buffer, sems)
    own = split(own_ref[...])
    gram = dot_split(own, own, NT)
    for i in range(pieces):
        await_fetch(vcs[i], buffer, sems, i)
    total = None
    for i in range(pieces):
        term = dot_split(split(buffer[table[3, i]]), split(pcs[i][...]), NT)
        total = term if total is None else total + term
    block_row = lax.broadcasted_iota(jnp.int32, gram.shape, 0) // nb
    block_col = lax.broadcasted_iota(jnp.int32, gram.shape, 1) // nb
    out_ref[...] = jnp.where(block_row > block_col, gram, total)


def inner_products(table, own, vcs, pcs, nb):
    pieces = len(vcs)
    vectors, width = vcs[0].shape
    vmem = pl.BlockSpec(memory_space=pltpu.VMEM)
    return pl.pallas_call(
        functools.partial(inner_kernel, pieces, nb),
        out_shape=jax.ShapeDtypeStruct((vectors, vectors), F32),
        in_specs=[pl.BlockSpec(memory_space=pltpu.SMEM), vmem] + anywhere(pieces) + [vmem] * pieces,
        scratch_shapes=[pltpu.VMEM((pieces, vectors, width), F32), pltpu.SemaphoreType.DMA((pieces,))],
        compiler_params=params(),
        cost_estimate=cost(6 * (pieces + 1) * vectors * vectors * width, 8 * pieces * vectors * width),
        name="inner_products",
    )(table, own, *vcs, *pcs)


def coefficients_kernel(panels, blocks_ref, turned_ref, factor_ref, factor_t_ref, a_ref, b_ref, cross_ref):
    a_ref[...] = jnp.zeros_like(a_ref)
    b_ref[...] = jnp.zeros_like(b_ref)
    for p in range(panels):
        inner = turned_ref[p, p]
        for q in range(p):
            total = None
            for i in range(q + 1):
                term = dot_full(turned_ref[p, i], a_ref[q, i], NT) + dot_full(blocks_ref[p, i], b_ref[q, i], NT)
                total = term if total is None else total + term
            cross_ref[q] = total
            inner = inner - (dot_full(blocks_ref[p, q], total, NT) + dot_full(total, blocks_ref[p, q], NT))
        for i in range(p):
            a_sum, b_sum = None, None
            for q in range(i, p):
                term = dot_full(blocks_ref[p, q], a_ref[q, i])
                a_sum = term if a_sum is None else a_sum + term
                term = dot_full(blocks_ref[p, q], b_ref[q, i])
                b_sum = term if b_sum is None else b_sum + term
            a_ref[p, i] = -dot_full(factor_t_ref[p], a_sum)
            b_ref[p, i] = -dot_full(factor_t_ref[p], cross_ref[i] + b_sum)
        a_ref[p, p] = factor_t_ref[p]
        b_ref[p, p] = -0.5 * dot_full(factor_t_ref[p], dot_full(inner, factor_ref[p]))


def coefficients(inner, factor):
    panels, nb, _ = factor.shape
    size = -(-nb // LANES) * LANES
    grown = ((0, size - nb),) * 2
    blocks = inner.reshape(panels, nb, panels, nb).transpose(0, 2, 1, 3)
    blocks = jnp.pad(blocks, ((0, 0), (0, 0)) + grown)
    factor = jnp.pad(factor, ((0, 0),) + grown)
    shape = jax.ShapeDtypeStruct((panels, panels, size, size), F32)
    a, b = pl.pallas_call(
        functools.partial(coefficients_kernel, panels),
        out_shape=[shape, shape],
        in_specs=[pl.BlockSpec(memory_space=pltpu.VMEM)] * 4,
        scratch_shapes=[pltpu.VMEM((panels, size, size), F32)],
        compiler_params=pltpu.CompilerParams(vmem_limit_bytes=VMEM_LIMIT),
        name="coefficients",
    )(blocks, blocks.transpose(1, 0, 3, 2), factor, factor.transpose(0, 2, 1))
    whole = lambda value: value[..., :nb, :nb].transpose(0, 2, 1, 3).reshape(panels * nb, panels * nb)
    return whole(a), whole(b)


def update_kernel(count, pieces, width, table, a_ref, b_ref, m_ref, *refs):
    vcs, pcs, refs = refs[:pieces], refs[pieces : 2 * pieces], refs[2 * pieces :]
    vs, ps, refs = refs[:count], refs[count : 2 * count], refs[2 * count :]
    out_ref, buffer, v_buffer, p_buffer, wh, wl, xh, xl, sems, v_sems, p_sems = refs
    step = pl.program_id(0)

    @pl.when(step == 0)
    def _():
        fetch(vcs + pcs, buffer, sems)
        fetch(vs, v_buffer, v_sems)
        fetch(ps, p_buffer, p_sems)
        a = split(a_ref[...])
        b = split(b_ref[...] + b_ref[...].T)
        for i in range(2 * pieces):
            await_fetch(vcs[0], buffer, sems, i)
        for i in range(pieces):
            cols = pl.ds(pl.multiple_of(table[4, i] * width, width), width)
            v = split(buffer[table[5, i]])
            wh[:, cols], wl[:, cols] = split(dot_split(a, split(buffer[pieces + i]), NN) + dot_split(b, v, NN))
            xh[:, cols], xl[:, cols] = split(dot_split(a, v, TN))

    await_fetch(vs[0], v_buffer, v_sems, step)
    await_fetch(ps[0], p_buffer, p_sems, step)
    half = m_ref.shape[0] // 2
    for part in range(2):
        rows = pl.ds(part * half, half)
        v = split(v_buffer[step, :, rows].T)
        p = split(p_buffer[step, rows, :])
        for i in range(pieces):
            cols = pl.ds(i * width, width)
            term = dot_split(v, (wh[:, cols], wl[:, cols]), NN) + dot_split(p, (xh[:, cols], xl[:, cols]), NN)
            out_ref[rows, cols] = m_ref[rows, cols] - term


def update_matrix(table, a, b, vcs, pcs, vs, ps, matrix):
    pieces, count = len(vcs), len(vs)
    vectors, width = vcs[0].shape
    tile = vs[0].shape[1]
    cols = matrix.shape[1]
    whole = lambda *shape: pl.BlockSpec(shape, lambda s, t: (0,) * len(shape))
    here = pl.BlockSpec((tile, cols), lambda s, t: (t[0, s], 0))
    return pl.pallas_call(
        functools.partial(update_kernel, count, pieces, width),
        out_shape=jax.ShapeDtypeStruct(matrix.shape, F32),
        grid_spec=pltpu.PrefetchScalarGridSpec(
            num_scalar_prefetch=1,
            grid=(count,),
            in_specs=[whole(vectors, vectors), whole(vectors, vectors), here] + anywhere(2 * (pieces + count)),
            out_specs=here,
            scratch_shapes=[
                pltpu.VMEM((2 * pieces, vectors, width), F32),
                pltpu.VMEM((count, vectors, tile), F32),
                pltpu.VMEM((count, tile, vectors), F32),
            ]
            + [pltpu.VMEM((vectors, cols), BF16)] * 4
            + [pltpu.SemaphoreType.DMA((n,)) for n in (2 * pieces, count, count)],
        ),
        compiler_params=params(),
        cost_estimate=cost(12 * count * tile * cols * vectors, 8 * count * tile * cols),
        name="update_matrix",
    )(table, a, b, matrix, *vcs, *pcs, *vs, *ps)


def total_over_all(value, row_count, col_count):
    value = value + exchange(value, 1, col_count)
    parity = lax.axis_index("col") % 2
    height = value.shape[0] // 2
    mine = lax.dynamic_slice_in_dim(value, parity * height, height, 0)
    bit = 2
    while bit < col_count:
        mine = mine + exchange(mine, bit, col_count)
        bit *= 2
    total = mine
    for shift in range(1, row_count):
        total = total + lax.ppermute(mine, "row", [(i, (i + shift) % row_count) for i in range(row_count)])
    other = exchange(total, 1, col_count)
    first = jnp.where(parity == 0, total, other)
    second = jnp.where(parity == 0, other, total)
    return jnp.concatenate([first, second], axis=0)


def shards(symmetric, reflectors, tri_factor):
    row_count = lax.axis_size("row")
    col_count = lax.axis_size("col")
    row = lax.axis_index("row")
    col = lax.axis_index("col")
    panels, nb, own_width = reflectors.shape
    vectors = panels * nb
    per_row = col_count // row_count
    pairs = col_count // 2

    ring = [0] + list(range(1, row_count, 2)) + list(range(2, row_count, 2))[::-1]
    ring_array = jnp.array(ring, jnp.int32)
    place_of = jnp.array([ring.index(i) for i in range(row_count)], jnp.int32)
    place = place_of[row]
    offsets = list(range(0, col_count, 2)) + list(range(1, col_count, 2))
    block = col // per_row
    steps = jnp.arange(row_count, dtype=jnp.int32)

    def padded(entries):
        return jnp.pad(entries, (0, col_count - entries.shape[0]))

    sent = ring_array[(place - 1 - steps) % row_count]
    gathered = ring_array[(place - steps) % row_count]
    table = jnp.stack(
        [
            col ^ jnp.array(offsets, jnp.int32),
            padded(sent),
            padded((block - steps) % row_count),
            padded((block - sent) % row_count),
            padded(gathered),
            padded((block - gathered) % row_count),
        ]
    ).astype(jnp.int32)

    own = reflectors.reshape(vectors, own_width)

    near = [own] + [exchange(own, offset, col_count) for offset in offsets[1:pairs]]
    far = [exchange(piece, 1, col_count) for piece in near]

    around = [own]
    for _ in range(row_count - 1):
        around.append(ring_shift(around[-1], ring))
    around, far = lax.optimization_barrier((around, far))
    vcs = []
    for k in range(row_count):
        target = [(j % row_count + k) % row_count * per_row + j // row_count for j in range(col_count)]
        wanted = (place - place_of[(col % row_count + k) % row_count]) % row_count
        piece = around[0]
        for i in range(1, row_count):
            piece = jnp.where(wanted == i, around[i], piece)
        vcs.append(lax.ppermute(piece, "col", list(enumerate(target))))

    partial = product_columns(table, near + far, symmetric, row_count)
    partial, vcs = lax.optimization_barrier((partial, vcs))

    total = partial[0]
    for i in range(1, row_count):
        total = ring_shift(total, ring) + partial[i]
    pcs = [total]
    for _ in range(row_count - 1):
        pcs.append(ring_shift(pcs[-1], ring))

    other = product_rows(table, pairs, pairs, vcs, symmetric)
    other = exchange(other, 1, col_count)
    mine = product_rows(table, 0, pairs, vcs, symmetric, (other,))

    share = inner_products(table, own, vcs, partial, nb)
    inner = total_over_all(share, row_count, col_count)
    a, b = coefficients(inner, tri_factor)

    total = mine[0]
    for i in range(1, pairs):
        total = total + exchange(mine[i], offsets[i], col_count)
    near_rows = [total] + [exchange(total, offset, col_count) for offset in offsets[1:pairs]]
    far_rows = [exchange(piece, 1, col_count) for piece in near_rows]

    return update_matrix(table, a, b, vcs, pcs, near + far, near_rows + far_rows, symmetric)


def solution(mesh):
    placed = (P("row", "col"), P(None, None, ("row", "col")), P())
    return jax.shard_map(shards, mesh=mesh, in_specs=placed, out_specs=P("row", "col"), check_vma=False)
```

```python
import functools

import jax
import jax.numpy as jnp
from jax import lax
from jax.experimental import pallas as pl
from jax.experimental.pallas import tpu as pltpu
from jax.sharding import PartitionSpec as P


F32 = jnp.float32
BF16 = jnp.bfloat16
VMEM_LIMIT = 60 * 1024 * 1024
NN = ((1,), (0,))
NT = ((1,), (1,))
TN = ((0,), (0,))


def split(value):
    high = value.astype(BF16)
    return high, (value - high.astype(F32)).astype(BF16)


def dot_split(left, right, dims):
    def part(a, b):
        return lax.dot_general(a, b, (dims, ((), ())), preferred_element_type=F32)

    return part(left[0], right[0]) + (part(left[0], right[1]) + part(left[1], right[0]))


def params():
    return pltpu.CompilerParams(vmem_limit_bytes=VMEM_LIMIT)


def cost(flops, bytes_accessed):
    return pl.CostEstimate(flops=flops, bytes_accessed=bytes_accessed, transcendentals=0)


def anywhere(count):
    return [pl.BlockSpec(memory_space=pl.ANY)] * count


def exchange(value, offset, count):
    return lax.ppermute(value, "col", [(i, i ^ offset) for i in range(count)])


def ring_shift(value, ring):
    size = len(ring)
    return lax.ppermute(value, "row", [(ring[i], ring[(i + 1) % size]) for i in range(size)])


def fetch(refs, buffer, sems):
    for i, ref in enumerate(refs):
        pltpu.make_async_copy(ref, buffer.at[i], sems.at[i]).start()


def await_fetch(ref, buffer, sems, i):
    pltpu.make_async_copy(ref, buffer.at[i], sems.at[i]).wait()


def columns_kernel(count, pieces, width, more, table, *refs):
    vs, m_ref, refs = refs[:count], refs[count], refs[count + 1 :]
    before, outs, (buffer, sems) = refs[:more], refs[more : more + pieces], refs[-2:]
    step = pl.program_id(0)

    @pl.when(step == 0)
    def _():
        fetch(vs, buffer, sems)

    await_fetch(vs[0], buffer, sems, step)
    left = split(buffer[step])
    for i in range(pieces):
        at = pl.multiple_of(table[1, i] * width, width)
        total = dot_split(left, split(m_ref[:, pl.ds(at, width)]), NN)

        @pl.when(step == 0)
        def _():
            outs[i][...] = total + before[i][...] if more else total

        @pl.when(step > 0)
        def _():
            outs[i][...] += total


def product_columns(table, first, vs, matrix, pieces, before=()):
    count = len(vs)
    vectors, tile = vs[0].shape
    cols = matrix.shape[1]
    width = cols // pieces
    piece = pl.BlockSpec((vectors, width), lambda s, t: (0, 0))
    return pl.pallas_call(
        functools.partial(columns_kernel, count, pieces, width, len(before)),
        out_shape=[jax.ShapeDtypeStruct((vectors, width), F32)] * pieces,
        grid_spec=pltpu.PrefetchScalarGridSpec(
            num_scalar_prefetch=1,
            grid=(count,),
            in_specs=anywhere(count)
            + [pl.BlockSpec((tile, cols), lambda s, t: (t[0, first + s], 0))]
            + [piece] * len(before),
            out_specs=[piece] * pieces,
            scratch_shapes=[pltpu.VMEM((count, vectors, tile), F32), pltpu.SemaphoreType.DMA((count,))],
        ),
        compiler_params=params(),
        cost_estimate=cost(6 * count * tile * cols * vectors, 4 * count * tile * cols),
        name="product_columns",
    )(table, *vs, matrix, *before)


def rows_kernel(pieces, width, more, table, *refs):
    vcs, refs = refs[:pieces], refs[pieces:]
    m_ref, refs = refs[0], refs[1:]
    before, (out_ref, buffer, high_ref, low_ref, sems) = refs[:more], refs[more:]

    @pl.when(pl.program_id(0) == 0)
    def _():
        fetch(vcs, buffer, sems)
        for k in range(pieces):
            await_fetch(vcs[k], buffer, sems, k)
            high_ref[k], low_ref[k] = split(buffer[k])

    total = before[0][0] if more else None
    for k in range(pieces):
        at = pl.multiple_of(table[2, k] * width, width)
        left = split(m_ref[:, pl.ds(at, width)])
        term = dot_split(left, (high_ref[k], low_ref[k]), NT)
        total = term if total is None else total + term
    out_ref[0] = total


def product_rows(table, first, count, vcs, matrix, before=()):
    pieces = len(vcs)
    vectors, width = vcs[0].shape
    rows, cols = matrix.shape
    tile = rows // (2 * count)
    entry = pl.BlockSpec((1, tile, vectors), lambda s, t: (s, 0, 0))
    return pl.pallas_call(
        functools.partial(rows_kernel, pieces, width, len(before)),
        out_shape=jax.ShapeDtypeStruct((count, tile, vectors), F32),
        grid_spec=pltpu.PrefetchScalarGridSpec(
            num_scalar_prefetch=1,
            grid=(count,),
            in_specs=anywhere(pieces)
            + [pl.BlockSpec((tile, cols), lambda s, t: (t[0, first + s], 0))]
            + [entry] * len(before),
            out_specs=entry,
            scratch_shapes=[pltpu.VMEM((pieces, vectors, width), F32)]
            + [pltpu.VMEM((pieces, vectors, width), BF16)] * 2
            + [pltpu.SemaphoreType.DMA((pieces,))],
        ),
        compiler_params=params(),
        cost_estimate=cost(6 * count * tile * cols * vectors, 4 * count * tile * cols),
        name="product_rows",
    )(table, *vcs, matrix, *before)


def inner_kernel(pieces, nb, table, own_ref, *refs):
    vcs, pcs, out_ref = refs[:pieces], refs[pieces : 2 * pieces], refs[2 * pieces]
    buffer, sems = refs[2 * pieces + 1 :]
    fetch(vcs, buffer, sems)
    own = split(own_ref[...])
    gram = dot_split(own, own, NT)
    for i in range(pieces):
        await_fetch(vcs[i], buffer, sems, i)
    total = None
    for i in range(pieces):
        term = dot_split(split(buffer[table[3, i]]), split(pcs[i][...]), NT)
        total = term if total is None else total + term
    block_row = lax.broadcasted_iota(jnp.int32, gram.shape, 0) // nb
    block_col = lax.broadcasted_iota(jnp.int32, gram.shape, 1) // nb
    out_ref[...] = jnp.where(block_row > block_col, gram, total)


def inner_products(table, own, vcs, pcs, nb):
    pieces = len(vcs)
    vectors, width = vcs[0].shape
    vmem = pl.BlockSpec(memory_space=pltpu.VMEM)
    return pl.pallas_call(
        functools.partial(inner_kernel, pieces, nb),
        out_shape=jax.ShapeDtypeStruct((vectors, vectors), F32),
        in_specs=[pl.BlockSpec(memory_space=pltpu.SMEM), vmem] + anywhere(pieces) + [vmem] * pieces,
        scratch_shapes=[pltpu.VMEM((pieces, vectors, width), F32), pltpu.SemaphoreType.DMA((pieces,))],
        compiler_params=params(),
        cost_estimate=cost(6 * (pieces + 1) * vectors * vectors * width, 8 * pieces * vectors * width),
        name="inner_products",
    )(table, own, *vcs, *pcs)


def coefficients_kernel(panels, inner_ref, factor_ref, a_out, b_out, a_ref, b_ref, blocks_ref, turned_ref, cross_ref):
    nb = factor_ref.shape[1]

    def dot(left, right, dims=NN):
        return dot_split(split(left), split(right), dims)

    def place(p, i):
        return slice(p * nb, (p + 1) * nb), slice(i * nb, (i + 1) * nb)

    for p in range(panels):
        for i in range(panels):
            block = inner_ref[place(p, i)]
            if p > i:
                blocks_ref[p, i] = block
            else:
                turned_ref[i, p] = block.T
    a_out[...] = jnp.zeros_like(a_out)
    b_out[...] = jnp.zeros_like(b_out)
    for p in range(panels):
        factor_t = factor_ref[p].T
        inner = turned_ref[p, p]
        for q in range(p):
            total = None
            for i in range(q + 1):
                term = dot(turned_ref[p, i], a_ref[q, i], NT) + dot(blocks_ref[p, i], b_ref[q, i], NT)
                total = term if total is None else total + term
            cross_ref[q] = total
            inner = inner - (dot(blocks_ref[p, q], total, NT) + dot(total, blocks_ref[p, q], NT))
        for i in range(p):
            a_sum, b_sum = None, None
            for q in range(i, p):
                term = dot(blocks_ref[p, q], a_ref[q, i])
                a_sum = term if a_sum is None else a_sum + term
                term = dot(blocks_ref[p, q], b_ref[q, i])
                b_sum = term if b_sum is None else b_sum + term
            a_ref[p, i] = -dot(factor_t, a_sum)
            b_ref[p, i] = -dot(factor_t, cross_ref[i] + b_sum)
        a_ref[p, p] = factor_t
        b_ref[p, p] = -0.5 * dot(factor_t, dot(inner, factor_ref[p]))
    for p in range(panels):
        for i in range(p + 1):
            a_out[place(p, i)] = a_ref[p, i]
            b_out[place(p, i)] = b_ref[p, i]


def coefficients(inner, factor):
    panels, nb, _ = factor.shape
    shape = jax.ShapeDtypeStruct(inner.shape, F32)
    return pl.pallas_call(
        functools.partial(coefficients_kernel, panels),
        out_shape=[shape, shape],
        in_specs=[pl.BlockSpec(memory_space=pltpu.VMEM)] * 2,
        scratch_shapes=[pltpu.VMEM((panels, panels, nb, nb), F32)] * 4 + [pltpu.VMEM((panels, nb, nb), F32)],
        compiler_params=params(),
        name="coefficients",
    )(inner, factor)


def update_kernel(count, pieces, width, table, a_ref, b_ref, m_ref, *refs):
    vcs, pcs, refs = refs[:pieces], refs[pieces : 2 * pieces], refs[2 * pieces :]
    vs, ps, refs = refs[:count], refs[count : 2 * count], refs[2 * count :]
    out_ref, buffer, v_buffer, p_buffer, wh, wl, xh, xl, sems, v_sems, p_sems = refs
    step = pl.program_id(0)

    @pl.when(step == 0)
    def _():
        fetch(vcs + pcs, buffer, sems)
        fetch(vs, v_buffer, v_sems)
        fetch(ps, p_buffer, p_sems)
        a = split(a_ref[...])
        b = split(b_ref[...] + b_ref[...].T)
        for i in range(2 * pieces):
            await_fetch(vcs[0], buffer, sems, i)
        for i in range(pieces):
            cols = pl.ds(pl.multiple_of(table[4, i] * width, width), width)
            v = split(buffer[table[5, i]])
            wh[:, cols], wl[:, cols] = split(dot_split(a, split(buffer[pieces + i]), NN) + dot_split(b, v, NN))
            xh[:, cols], xl[:, cols] = split(dot_split(a, v, TN))

    await_fetch(vs[0], v_buffer, v_sems, step)
    await_fetch(ps[0], p_buffer, p_sems, step)
    half = m_ref.shape[0] // 2
    for part in range(2):
        rows = pl.ds(part * half, half)
        v = split(v_buffer[step, :, rows].T)
        p = split(p_buffer[step, rows, :])
        for i in range(pieces):
            cols = pl.ds(i * width, width)
            term = dot_split(v, (wh[:, cols], wl[:, cols]), NN) + dot_split(p, (xh[:, cols], xl[:, cols]), NN)
            out_ref[rows, cols] = m_ref[rows, cols] - term


def update_matrix(table, a, b, vcs, pcs, vs, ps, matrix):
    pieces, count = len(vcs), len(vs)
    vectors, width = vcs[0].shape
    tile = vs[0].shape[1]
    cols = matrix.shape[1]
    whole = lambda *shape: pl.BlockSpec(shape, lambda s, t: (0,) * len(shape))
    here = pl.BlockSpec((tile, cols), lambda s, t: (t[0, s], 0))
    return pl.pallas_call(
        functools.partial(update_kernel, count, pieces, width),
        out_shape=jax.ShapeDtypeStruct(matrix.shape, F32),
        grid_spec=pltpu.PrefetchScalarGridSpec(
            num_scalar_prefetch=1,
            grid=(count,),
            in_specs=[whole(vectors, vectors), whole(vectors, vectors), here] + anywhere(2 * (pieces + count)),
            out_specs=here,
            scratch_shapes=[
                pltpu.VMEM((2 * pieces, vectors, width), F32),
                pltpu.VMEM((count, vectors, tile), F32),
                pltpu.VMEM((count, tile, vectors), F32),
            ]
            + [pltpu.VMEM((vectors, cols), BF16)] * 4
            + [pltpu.SemaphoreType.DMA((n,)) for n in (2 * pieces, count, count)],
        ),
        compiler_params=params(),
        cost_estimate=cost(12 * count * tile * cols * vectors, 8 * count * tile * cols),
        name="update_matrix",
    )(table, a, b, matrix, *vcs, *pcs, *vs, *ps)


def total_over_all(value, row_count, col_count):
    value = value + exchange(value, 1, col_count)
    parity = lax.axis_index("col") % 2
    height = value.shape[0] // 2
    mine = lax.dynamic_slice_in_dim(value, parity * height, height, 0)
    bit = 2
    while bit < col_count:
        mine = mine + exchange(mine, bit, col_count)
        bit *= 2
    total = mine
    for shift in range(1, row_count):
        total = total + lax.ppermute(mine, "row", [(i, (i + shift) % row_count) for i in range(row_count)])
    other = exchange(total, 1, col_count)
    first = jnp.where(parity == 0, total, other)
    second = jnp.where(parity == 0, other, total)
    return jnp.concatenate([first, second], axis=0)


def shards(symmetric, reflectors, tri_factor):
    row_count = lax.axis_size("row")
    col_count = lax.axis_size("col")
    row = lax.axis_index("row")
    col = lax.axis_index("col")
    panels, nb, own_width = reflectors.shape
    vectors = panels * nb
    per_row = col_count // row_count
    pairs = col_count // 2

    ring = [0] + list(range(1, row_count, 2)) + list(range(2, row_count, 2))[::-1]
    ring_array = jnp.array(ring, jnp.int32)
    place_of = jnp.array([ring.index(i) for i in range(row_count)], jnp.int32)
    place = place_of[row]
    offsets = list(range(0, col_count, 2)) + list(range(1, col_count, 2))
    block = col // per_row
    steps = jnp.arange(row_count, dtype=jnp.int32)

    def padded(entries):
        return jnp.pad(entries, (0, col_count - entries.shape[0]))

    sent = ring_array[(place - 1 - steps) % row_count]
    gathered = ring_array[(place - steps) % row_count]
    table = jnp.stack(
        [
            col ^ jnp.array(offsets, jnp.int32),
            padded(sent),
            padded((block - steps) % row_count),
            padded((block - sent) % row_count),
            padded(gathered),
            padded((block - gathered) % row_count),
        ]
    ).astype(jnp.int32)

    own = reflectors.reshape(vectors, own_width)

    near = [own] + [exchange(own, offset, col_count) for offset in offsets[1:pairs]]
    far = [exchange(piece, 1, col_count) for piece in near]

    around = [own]
    for _ in range(row_count - 1):
        around.append(ring_shift(around[-1], ring))
    vcs = []
    for k in range(row_count):
        target = [(j % row_count + k) % row_count * per_row + j // row_count for j in range(col_count)]
        wanted = (place - place_of[(col % row_count + k) % row_count]) % row_count
        piece = around[0]
        for i in range(1, row_count):
            piece = jnp.where(wanted == i, around[i], piece)
        vcs.append(lax.ppermute(piece, "col", list(enumerate(target))))

    partial = product_columns(table, 0, near, symmetric, row_count)
    partial = product_columns(table, pairs, far, symmetric, row_count, partial)
    partial, vcs = lax.optimization_barrier((partial, vcs))

    total = partial[0]
    for i in range(1, row_count):
        total = ring_shift(total, ring) + partial[i]
    pcs = [total]
    for _ in range(row_count - 1):
        pcs.append(ring_shift(pcs[-1], ring))

    other = product_rows(table, pairs, pairs, vcs, symmetric)
    other = exchange(other, 1, col_count)
    mine = product_rows(table, 0, pairs, vcs, symmetric, (other,))

    share = inner_products(table, own, vcs, partial, nb)
    inner = total_over_all(share, row_count, col_count)
    a, b = coefficients(inner, tri_factor)

    total = mine[0]
    for i in range(1, pairs):
        total = total + exchange(mine[i], offsets[i], col_count)
    near_rows = [total]
    for i in range(1, pairs):
        near_rows.append(exchange(total, offsets[i], col_count))
    far_rows = [exchange(piece, 1, col_count) for piece in near_rows]

    return update_matrix(table, a, b, vcs, pcs, near + far, near_rows + far_rows, symmetric)


def solution(mesh):
    placed = (P("row", "col"), P(None, None, ("row", "col")), P())
    return jax.shard_map(shards, mesh=mesh, in_specs=placed, out_specs=P("row", "col"), check_vma=False)
```
